512 devices in a mesh: station: 32 (over x, y, core), section: 16 (over z).
Axes of the slice: x: 4, y: 4, z: 16, core: 2. Of those that a mesh axis runs over, the one named last changes fastest.
Arguments:
- voltages: bfloat16 [32, 512, 17408], P('station', 'section'), may hold values from -6 to 6
- taper: float32 [14, 1024], replicated, may hold values from -1.6 to 1.6
- beam_weight_table: bfloat16 [32, 8, 512, 2, 512], P('station', None, 'section'), may hold values from -0.5 to 0.5
- starts: int32 [8], replicated, may hold values from 0 to 15
- owner_map: int32 [512], replicated, may hold values from 0 to 31, as said below
Outputs:
- visibilities: bfloat16 [16, 32, 1, 8, 4, 64, 128], P('section', 'station')
The draws below stay inside these ranges and needn't reach their ends.
Inputs may be any that keep to these rules, and one draw needn't show every extreme that they name: `owner_map`: within each block of 32 consecutive channels every owner 0 to 31 owns exactly 1 channels.
All inputs are finite; a program needn't handle non-finite values.
Results may differ from the reference program's by a relative error of at most 0.014.
Values may be sent and summed in bfloat16 or wider, within the bound.
No kernel may reach another device: no remote copies, remote signals or barrier semaphores. Data moves between devices by JAX's collectives and lax.ppermute only.
A program may use at most 64 MiB of HBM per device.

```python
import math
import jax
import jax.numpy as jnp
from jax import lax

NFFT = 1024
TAPS = 14
BEAM_TOTAL = 8
SECTION_ANTENNAS = 16
FRAMES = 4
FREQ_CHANNELS = 512
STATION_SECTIONS = 16
ARRAY_STATIONS = 32
STATION_ANTENNAS = 256
SIGNAL_INPUTS = 512
SAMPLES = 17408
SPAN = 8
CPO = 1


def draw_owner_map(key, part):
    block = FREQ_CHANNELS // STATION_SECTIONS
    several = jax.random.split(key, STATION_SECTIONS)
    orders = jax.vmap(lambda single: jax.random.permutation(single, block))(several)
    return (orders // CPO).reshape(FREQ_CHANNELS).astype(jnp.int32)


def set_ends(drawn, stream_key, smallest, top_value):
    longest = drawn.shape.index(max(drawn.shape))
    spots = []
    for shift in (0, 1):
        where = [jax.random.randint(jax.random.fold_in(stream_key, axis), (), 0, length) for axis, length in enumerate(drawn.shape)]
        where[longest] = (where[longest] + shift) % drawn.shape[longest]
        spots.append(tuple(where))
    return drawn.at[spots[0]].set(smallest).at[spots[1]].set(top_value)


def steps_of(own_key, shape, pieces, smallest, largest):
    gain = 1.0
    for axis_at, parts in pieces:
        heights = jax.random.uniform(jax.random.fold_in(jax.random.fold_in(own_key, 6), axis_at), (parts,), jnp.float32, smallest / len(pieces), largest / len(pieces))
        gain = gain * jnp.repeat(jnp.exp(heights), shape[axis_at] // parts).reshape((-1,) + (1,) * (len(shape) - 1 - axis_at))
    return gain


def gaussian(rng, dims, scale, bound, cuts=(), kind=jnp.bfloat16):
    array = scale * jax.random.normal(rng, dims, jnp.float32)
    if cuts:
        array = array * steps_of(rng, dims, cuts, -0.22, 0.18)
    return jnp.clip(array, -bound, bound).astype(kind)


def setup_inputs(seed: int = 0) -> dict:
    streams_of = jax.random.split(jax.random.key(seed), 6)
    voltages = gaussian(streams_of[0], (ARRAY_STATIONS, SIGNAL_INPUTS, SAMPLES), 1.0, 6.0, ((0, 32), (1, 16)))
    taper = gaussian(streams_of[1], (TAPS, NFFT), 0.27, 1.6, (), jnp.float32)
    beam_weight_table = gaussian(streams_of[2], (ARRAY_STATIONS, BEAM_TOTAL, SIGNAL_INPUTS, 2, FREQ_CHANNELS), (SECTION_ANTENNAS * STATION_SECTIONS // 2) ** -0.5, 0.5, ((0, 32), (2, 16)))
    starts = set_ends(jax.random.randint(streams_of[3], (BEAM_TOTAL,), 0, STATION_SECTIONS), jax.random.fold_in(streams_of[3], 1), 0, STATION_SECTIONS - 1).astype(jnp.int32)
    owner_map = draw_owner_map(jax.random.fold_in(streams_of[5], 71), 0)
    return {"voltages": voltages, "taper": taper, "beam_weight_table": beam_weight_table, "starts": starts, "owner_map": owner_map}


def dft_table():
    index_n = jnp.arange(NFFT, dtype=jnp.int32)[:, None]
    index_k = jnp.arange(FREQ_CHANNELS, dtype=jnp.int32)[None, :]
    phase = (index_n * index_k % NFFT).astype(jnp.float32) * (2.0 * math.pi / NFFT)
    factor = 1.0 / math.sqrt(NFFT)
    return jnp.concatenate([jnp.cos(phase) * factor, -jnp.sin(phase) * factor], axis=1).astype(jnp.bfloat16)

def station_beams(volts, weights, inside, taper, table):
    framed = volts.reshape(SIGNAL_INPUTS, FRAMES + TAPS - 1, NFFT)
    filtered = jnp.zeros((SIGNAL_INPUTS, FRAMES, NFFT), jnp.float32)
    for tap in range(TAPS):
        filtered = filtered + taper[tap][None, None, :] * framed[:, tap:tap + FRAMES, :].astype(jnp.float32)
    rows = filtered.astype(jnp.bfloat16).reshape(SIGNAL_INPUTS * FRAMES, NFFT)
    spectra = jnp.dot(rows, table, preferred_element_type=jnp.float32)
    spectra = spectra.reshape(STATION_ANTENNAS, 2, FRAMES, 2, FREQ_CHANNELS)
    real_x = spectra[:, :, :, 0, :]
    imag_x = spectra[:, :, :, 1, :]
    scaled = weights.astype(jnp.float32).reshape(BEAM_TOTAL, STATION_ANTENNAS, 2, 2, FREQ_CHANNELS) * inside[:, :, None, None, None]
    real_w = scaled[:, :, :, 0, :]
    imag_w = scaled[:, :, :, 1, :]
    real_b = jnp.einsum('bapk,apfk->kbpf', real_w, real_x) - jnp.einsum('bapk,apfk->kbpf', imag_w, imag_x)
    imag_b = jnp.einsum('bapk,apfk->kbpf', real_w, imag_x) + jnp.einsum('bapk,apfk->kbpf', imag_w, real_x)
    return jnp.stack([real_b, imag_b], axis=3).astype(jnp.bfloat16)

def correlate(pair):
    real_z, imag_z = pair
    real_v = jnp.einsum('bfi,bfj->bfij', real_z, real_z) + jnp.einsum('bfi,bfj->bfij', imag_z, imag_z)
    imag_v = jnp.einsum('bfi,bfj->bfij', imag_z, real_z) - jnp.einsum('bfi,bfj->bfij', real_z, imag_z)
    return jnp.concatenate([real_v, imag_v], axis=-1).astype(jnp.bfloat16)

def reference(voltages, taper, beam_weight_table, starts, owner_map):
    table = dft_table()
    section_lookup = jnp.arange(STATION_ANTENNAS, dtype=jnp.int32) // SECTION_ANTENNAS
    offset = jnp.remainder(section_lookup[None, :] - starts[:, None], STATION_SECTIONS)
    inside = (offset < SPAN).astype(jnp.float32)

    def one_station(pair):
        return station_beams(pair[0], pair[1], inside, taper, table)
    beams = lax.map(one_station, (voltages, beam_weight_table))
    block = FREQ_CHANNELS // STATION_SECTIONS
    ranked = jnp.argsort(owner_map.reshape(STATION_SECTIONS, block), axis=1, stable=True).astype(jnp.int32)
    ranked = (ranked + jnp.arange(STATION_SECTIONS, dtype=jnp.int32)[:, None] * block).reshape(FREQ_CHANNELS)
    picked = jnp.take(beams, ranked, axis=1)
    picked = jnp.transpose(picked, (1, 2, 5, 0, 3, 4)).astype(jnp.float32)
    real_z = picked[..., 0].reshape(FREQ_CHANNELS, BEAM_TOTAL, FRAMES, 2 * ARRAY_STATIONS)
    imag_z = picked[..., 1].reshape(FREQ_CHANNELS, BEAM_TOTAL, FRAMES, 2 * ARRAY_STATIONS)
    visible = lax.map(correlate, (real_z, imag_z))
    return visible.reshape(STATION_SECTIONS, ARRAY_STATIONS, CPO, BEAM_TOTAL, FRAMES, 2 * ARRAY_STATIONS, 4 * ARRAY_STATIONS)
```

```python
import functools
import math

import jax
import jax.numpy as jnp
import ml_dtypes
import numpy as np
from jax import lax
from jax.experimental import pallas as pl
from jax.experimental.pallas import tpu as pltpu
from jax.sharding import PartitionSpec as P

LANES = 128
F32 = jnp.float32
BF16 = jnp.bfloat16


def dft_table(length):
    half = length // 2
    n = np.arange(length, dtype=np.int32)[:, None]
    k = np.arange(half, dtype=np.int32)[None, :]
    phase = (n * k % length).astype(np.float32) * np.float32(2.0 * math.pi / length)
    factor = np.float32(1.0 / math.sqrt(length))
    real = (np.cos(phase) * factor).reshape(length, half // LANES, LANES)
    imag = (-np.sin(phase) * factor).reshape(length, half // LANES, LANES)
    return np.concatenate([real, imag], axis=2).reshape(length, length).astype(ml_dtypes.bfloat16)


def front_kernel(
    dims, starts_ref, section_ref, owner_ref, taper_ref, volts_hbm, weights_hbm, table_hbm,
    out_ref, volts, weights, table, rows, beams, sems,
):
    inputs, taps, frames, length, beam_count, sections, stations = dims
    channels = length // 2
    chunks = channels // LANES
    block = channels // sections
    half = 16
    parts = inputs // half
    volt_copies = [
        pltpu.make_async_copy(
            volts_hbm.at[0, pl.ds(i * half, half)], volts.at[pl.ds(i * half, half)], sems.at[i]
        )
        for i in range(parts)
    ]
    table_copies = [
        pltpu.make_async_copy(
            table_hbm.at[:, pl.ds(c * 2 * LANES, 2 * LANES)], table.at[c], sems.at[parts + c]
        )
        for c in range(chunks)
    ]
    weight_copy = pltpu.make_async_copy(weights_hbm, weights, sems.at[parts + chunks])
    for copy in volt_copies + table_copies:
        copy.start()
    weight_copy.start()

    for i in range(parts):
        volt_copies[i].wait()
        for c in range(length // LANES):
            at = c * LANES
            taper = [
                jnp.broadcast_to(taper_ref[pl.ds(t, 1), pl.ds(at, LANES)], (half, LANES))
                for t in range(taps)
            ]
            sums = [None] * frames
            for g in range(frames + taps - 1):
                value = volts[pl.ds(i * half, half), pl.ds(g * length + at, LANES)].astype(F32)
                for f in range(frames):
                    t = g - f
                    if 0 <= t < taps:
                        term = taper[t] * value
                        sums[f] = term if sums[f] is None else sums[f] + term
            for f in range(frames):
                rows[pl.ds(f * inputs + i * half, half), pl.ds(at, LANES)] = sums[f].astype(BF16)

    section = section_ref[0]
    keep = [
        jnp.where(((section - starts_ref[b] + sections) & (sections - 1)) < sections // 2, 1.0, 0.0)
        for b in range(beam_count)
    ]
    row = lax.broadcasted_iota(jnp.int32, (8, LANES), 0)
    low = row < 4
    first = (row & 2) == 0
    tiles = inputs // 8

    def tile_of(array, start):
        return lax.slice(array, (start, 0), (start + 8, LANES))

    for c in range(chunks):
        table_copies[c].wait()
        spectra = jnp.dot(rows[...], table[c], preferred_element_type=F32)
        real_x = lax.slice(spectra, (0, 0), (frames * inputs, LANES))
        imag_x = lax.slice(spectra, (0, LANES), (frames * inputs, 2 * LANES))
        if c == 0:
            weight_copy.wait()
        for b in range(beam_count):
            real_w = weights[b, 0, :, pl.ds(c * LANES, LANES)].astype(F32)
            imag_w = weights[b, 1, :, pl.ds(c * LANES, LANES)].astype(F32)
            sums = [[], []]
            for f in range(frames):
                real = imag = None
                for i in range(tiles):
                    xr = tile_of(real_x, f * inputs + i * 8)
                    xi = tile_of(imag_x, f * inputs + i * 8)
                    wr = tile_of(real_w, i * 8)
                    wi = tile_of(imag_w, i * 8)
                    re = wr * xr - wi * xi
                    im = wr * xi + wi * xr
                    real = re if real is None else real + re
                    imag = im if imag is None else imag + im
                sums[0].append(real)
                sums[1].append(imag)
            for part in range(2):
                v = sums[part]
                pairs = []
                for one, two in ((v[0], v[1]), (v[2], v[3])):
                    pairs.append(
                        jnp.where(low, one, two) + pltpu.roll(jnp.where(low, two, one), 4, 0)
                    )
                one = pairs[0] + pltpu.roll(pairs[0], 6, 0)
                two = pairs[1] + pltpu.roll(pairs[1], 2, 0)
                beams[pl.ds(b * 16 + part * 8, 8), pl.ds(c * LANES, LANES)] = (
                    jnp.where(first, one, two) * keep[b]
                )

    per = LANES // block
    for c in range(chunks):
        owners = owner_ref[pl.ds(0, 1), pl.ds(c * LANES, LANES)]
        lane = lax.broadcasted_iota(jnp.int32, (1, LANES), 1)
        target = (lane // block) * block + owners
        slot = lax.broadcasted_iota(jnp.int32, (LANES, LANES), 0)
        pick = jnp.where(slot == target, 1.0, 0.0).astype(BF16)
        values = beams[:, pl.ds(c * LANES, LANES)].astype(BF16)
        placed = lax.dot_general(
            pick, values, (((1,), (1,)), ((), ())), preferred_element_type=F32
        ).astype(BF16)
        for s in range(per):
            out_ref[c * per + s] = lax.slice(placed, (s * block, 0), ((s + 1) * block, LANES))


def place_of(beam, frame, part, pol):
    return beam * 16 + part * 8 + (frame & 1) * 4 + (frame >> 1) * 2 + pol


def selectors(beam_count, frames, stations):
    pairs = beam_count * frames
    pick = np.zeros((4 * pairs, LANES), np.float32)
    columns = np.zeros((2, LANES, 2 * pairs), np.float32)
    for b in range(beam_count):
        for f in range(frames):
            for part in range(2):
                for pol in range(2):
                    j = place_of(b, f, part, pol)
                    pick[(part * 2 + pol) * pairs + b * frames + f, j] = 1
                    columns[pol, j, part * pairs + b * frames + f] = 1
    spread = np.zeros((2, stations, 2 * stations), np.float32)
    for st in range(stations):
        for pol in range(2):
            spread[pol, st, 2 * st + pol] = 1
    zero = np.zeros_like(spread)
    left = np.concatenate([spread, zero], axis=2)
    right = np.concatenate([zero, spread], axis=2)
    first = np.stack([left, -right])
    second = np.stack([right, left])
    rows = np.stack([first, second])
    as_type = lambda a: a.astype(ml_dtypes.bfloat16)
    return as_type(pick), as_type(columns), as_type(np.swapaxes(spread, 1, 2)), as_type(rows)


def back_kernel(dims, z_ref, pick_ref, columns_ref, spread_ref, rows_ref, out_hbm, out, sems):
    beam_count, frames, stations = dims
    pairs = beam_count * frames
    z = z_ref[...].astype(BF16)
    turned = lax.dot_general(
        pick_ref[...], z, (((1,), (1,)), ((), ())), preferred_element_type=F32
    ).astype(BF16)
    row_values = []
    for kind in range(2):
        total = None
        for part in range(2):
            for pol in range(2):
                at = (part * 2 + pol) * pairs
                term = jnp.dot(
                    lax.slice(turned, (at, 0), (at + pairs, stations)),
                    rows_ref[kind, part, pol],
                    preferred_element_type=F32,
                )
                total = term if total is None else total + term
        row_values.append(total)
    column = None
    for pol in range(2):
        chosen = jnp.dot(z, columns_ref[pol], preferred_element_type=F32).astype(BF16)
        term = jnp.dot(spread_ref[pol], chosen, preferred_element_type=F32)
        column = term if column is None else column + term
    ends = []
    for b in range(beam_count):
        for f in range(frames):
            at = b * frames + f
            real = jnp.broadcast_to(
                lax.slice(column, (0, at), (2 * stations, at + 1)), (2 * stations, LANES)
            )
            imag = jnp.broadcast_to(
                lax.slice(column, (0, pairs + at), (2 * stations, pairs + at + 1)),
                (2 * stations, LANES),
            )
            one = lax.slice(row_values[0], (at, 0), (at + 1, LANES))
            two = lax.slice(row_values[1], (at, 0), (at + 1, LANES))
            out[b, f] = (real * one + imag * two).astype(BF16)
        copy = pltpu.make_async_copy(out.at[b], out_hbm.at[b], sems.at[b])
        copy.start()
        ends.append(copy)
    for copy in ends:
        copy.wait()


VMEM_SPEC = pl.BlockSpec(memory_space=pltpu.VMEM)
SMEM_SPEC = pl.BlockSpec(memory_space=pltpu.SMEM)
ANY_SPEC = pl.BlockSpec(memory_space=pl.ANY)


def front(sections, stations, starts, section, owner_map, taper, voltages, beam_weight_table):
    inputs = voltages.shape[1]
    taps, length = taper.shape
    frames = voltages.shape[2] // length - taps + 1
    channels = length // 2
    chunks = channels // LANES
    weights = jnp.transpose(beam_weight_table[0], (0, 2, 1, 3))
    dims = (inputs, taps, frames, length, weights.shape[0], sections, stations)
    return pl.pallas_call(
        functools.partial(front_kernel, dims),
        out_shape=jax.ShapeDtypeStruct((sections, channels // sections, LANES), BF16),
        in_specs=[SMEM_SPEC, SMEM_SPEC, VMEM_SPEC, VMEM_SPEC, ANY_SPEC, ANY_SPEC, ANY_SPEC],
        out_specs=VMEM_SPEC,
        scratch_shapes=[
            pltpu.VMEM((inputs, voltages.shape[2]), BF16),
            pltpu.VMEM(weights.shape, BF16),
            pltpu.VMEM((chunks, length, 2 * LANES), BF16),
            pltpu.VMEM((frames * inputs, length), BF16),
            pltpu.VMEM((LANES, channels), F32),
            pltpu.SemaphoreType.DMA((inputs // 16 + chunks + 1,)),
        ],
        name="front",
    )(
        starts, section, owner_map.reshape(1, channels), taper, voltages, weights,
        jnp.asarray(dft_table(length)),
    )


def back(beam_count, frames, z):
    stations = z.shape[0]
    shape = (beam_count, frames, 2 * stations, 4 * stations)
    matrices = [jnp.asarray(m) for m in selectors(beam_count, frames, stations)]
    return pl.pallas_call(
        functools.partial(back_kernel, (beam_count, frames, stations)),
        out_shape=jax.ShapeDtypeStruct(shape, BF16),
        in_specs=[VMEM_SPEC] * 5,
        out_specs=ANY_SPEC,
        scratch_shapes=[pltpu.VMEM(shape, BF16), pltpu.SemaphoreType.DMA((beam_count,))],
        name="back",
    )(z, *matrices)


def local(voltages, taper, beam_weight_table, starts, owner_map):
    sections = lax.axis_size("section")
    stations = lax.axis_size("station")
    section = lax.axis_index("section").astype(jnp.int32).reshape(1)
    partial = front(
        sections, stations, starts, section, owner_map, taper, voltages, beam_weight_table
    )
    arrived = lax.all_to_all(partial, "section", split_axis=0, concat_axis=0, tiled=True)
    complete = jnp.sum(arrived.astype(F32), axis=0)
    z = lax.all_to_all(
        complete.reshape(stations, 1, LANES), "station", split_axis=0, concat_axis=0, tiled=True
    ).reshape(stations, LANES)
    beam_count = beam_weight_table.shape[1]
    frames = voltages.shape[2] // taper.shape[1] - taper.shape[0] + 1
    visible = back(beam_count, frames, z)
    return visible.reshape(1, 1, 1, *visible.shape)


def solution(mesh):
    placed = (
        P("station", "section", None),
        P(),
        P("station", None, "section", None, None),
        P(),
        P(),
    )
    return jax.shard_map(
        local,
        mesh=mesh,
        in_specs=placed,
        out_specs=P("section", "station", None, None, None, None, None),
        check_vma=False,
    )
```

```python
import functools
import math

import jax
import jax.numpy as jnp
import ml_dtypes
import numpy as np
from jax import lax
from jax.experimental import pallas as pl
from jax.experimental.pallas import tpu as pltpu
from jax.sharding import PartitionSpec as P

LANES = 128
F32 = jnp.float32
BF16 = jnp.bfloat16


def dft_table(length):
    half = length // 2
    n = np.arange(length, dtype=np.int32)[:, None]
    k = np.arange(half, dtype=np.int32)[None, :]
    phase = (n * k % length).astype(np.float32) * np.float32(2.0 * math.pi / length)
    factor = np.float32(1.0 / math.sqrt(length))
    real = (np.cos(phase) * factor).reshape(length, half // LANES, LANES)
    imag = (-np.sin(phase) * factor).reshape(length, half // LANES, LANES)
    return np.concatenate([real, imag], axis=2).reshape(length, length).astype(ml_dtypes.bfloat16)


def front_kernel(
    dims, section_ref, starts_hbm, owner_hbm, taper_hbm, volts_hbm, weights_hbm, table_hbm,
    out_ref, starts, owner, taper, volts, weights, table, rows, gain, mixed, beams, sems,
):
    inputs, taps, frames, length, beam_count, sections, stations = dims
    channels = length // 2
    chunks = channels // LANES
    block = channels // sections
    half = 16
    parts = inputs // half
    starts_copy = pltpu.make_async_copy(starts_hbm, starts, sems.at[0])
    owner_copy = pltpu.make_async_copy(owner_hbm, owner, sems.at[1])
    taper_copy = pltpu.make_async_copy(taper_hbm, taper, sems.at[2])
    weight_copy = pltpu.make_async_copy(weights_hbm.at[0], weights, sems.at[3])
    volt_copies = [
        pltpu.make_async_copy(
            volts_hbm.at[0, pl.ds(i * half, half)], volts.at[pl.ds(i * half, half)], sems.at[4 + i]
        )
        for i in range(parts)
    ]
    table_copies = [
        pltpu.make_async_copy(
            table_hbm.at[:, pl.ds(c * 2 * LANES, 2 * LANES)], table.at[c], sems.at[4 + parts + c]
        )
        for c in range(chunks)
    ]
    copies = [taper_copy, *volt_copies, *table_copies[:1], weight_copy, *table_copies[1:]]
    for copy in copies + [starts_copy, owner_copy]:
        copy.start()

    taper_copy.wait()
    for i in range(parts):
        volt_copies[i].wait()
        for c in range(length // LANES):
            at = c * LANES
            gains = [
                jnp.broadcast_to(taper[pl.ds(t, 1), pl.ds(at, LANES)], (half, LANES))
                for t in range(taps)
            ]
            sums = [None] * frames
            for g in range(frames + taps - 1):
                value = volts[pl.ds(i * half, half), pl.ds(g * length + at, LANES)].astype(F32)
                for f in range(frames):
                    t = g - f
                    if 0 <= t < taps:
                        term = gains[t] * value
                        sums[f] = term if sums[f] is None else sums[f] + term
            for f in range(frames):
                rows[pl.ds(f * inputs + i * half, half), pl.ds(at, LANES)] = sums[f].astype(BF16)

    starts_copy.wait()
    section = section_ref[0]
    keep = [
        jnp.where(((section - starts[b] + sections) & (sections - 1)) < sections // 2, 1.0, 0.0)
        for b in range(beam_count)
    ]
    row = lax.broadcasted_iota(jnp.int32, (8, LANES), 0)
    low = row < 4
    even = (row & 1) == 0
    tiles = 2 * inputs // 8

    def spectra_of(c):
        table_copies[c].wait()
        spectra = jnp.dot(rows[...], table[c], preferred_element_type=F32)
        for f in range(frames):
            real = lax.slice(spectra, (f * inputs, 0), ((f + 1) * inputs, LANES))
            imag = lax.slice(spectra, (f * inputs, LANES), ((f + 1) * inputs, 2 * LANES))
            for at, one, two in ((0, real, -imag), (1, imag, real)):
                mixed[c % 2, at, f, pl.ds(0, inputs, stride=2), :] = one
                mixed[c % 2, at, f, pl.ds(1, inputs, stride=2), :] = two

    spectra_of(0)
    weight_copy.wait()
    for b in range(beam_count):
        gain[b] = weights[b].astype(F32).reshape(2 * inputs, channels)
    for c in range(chunks):
        if c + 1 < chunks:
            spectra_of(c + 1)
        for b in range(beam_count):
            gains = [gain[b, pl.ds(8 * i, 8), pl.ds(c * LANES, LANES)] for i in range(tiles)]
            for part in range(2):
                v = []
                for f in range(frames):
                    total = None
                    for i in range(tiles):
                        term = gains[i] * mixed[c % 2, part, f, pl.ds(8 * i, 8), :]
                        total = term if total is None else total + term
                    v.append(total)
                pairs = []
                for one, two in ((v[0], v[1]), (v[2], v[3])):
                    pairs.append(
                        jnp.where(low, one, two) + pltpu.roll(jnp.where(low, two, one), 4, 0)
                    )
                one = pairs[0] + pltpu.roll(pairs[0], 7, 0)
                two = pairs[1] + pltpu.roll(pairs[1], 1, 0)
                beams[pl.ds(b * 16 + part * 8, 8), pl.ds(c * LANES, LANES)] = (
                    jnp.where(even, one, two) * keep[b]
                )

    owner_copy.wait()
    per = LANES // block
    for c in range(chunks):
        owners = owner[pl.ds(0, 1), pl.ds(c * LANES, LANES)]
        lane = lax.broadcasted_iota(jnp.int32, (1, LANES), 1)
        target = (lane // block) * block + owners
        slot = lax.broadcasted_iota(jnp.int32, (LANES, LANES), 0)
        pick = jnp.where(slot == target, 1.0, 0.0).astype(BF16)
        values = beams[:, pl.ds(c * LANES, LANES)].astype(BF16)
        placed = lax.dot_general(
            pick, values, (((1,), (1,)), ((), ())), preferred_element_type=F32
        ).astype(BF16)
        for s in range(per):
            out_ref[c * per + s] = lax.slice(placed, (s * block, 0), ((s + 1) * block, LANES))


def place_of(beam, frame, part, pol):
    return beam * 16 + part * 8 + (frame & 1) * 4 + pol * 2 + (frame >> 1)


def selectors(beam_count, frames, stations):
    pairs = beam_count * frames
    pick = np.zeros((4 * pairs, LANES), np.float32)
    columns = np.zeros((2, LANES, 2 * pairs), np.float32)
    for b in range(beam_count):
        for f in range(frames):
            for part in range(2):
                for pol in range(2):
                    j = place_of(b, f, part, pol)
                    pick[(part * 2 + pol) * pairs + b * frames + f, j] = 1
                    columns[pol, j, part * pairs + b * frames + f] = 1
    spread = np.zeros((2, stations, 2 * stations), np.float32)
    for st in range(stations):
        for pol in range(2):
            spread[pol, st, 2 * st + pol] = 1
    zero = np.zeros_like(spread)
    left = np.concatenate([spread, zero], axis=2)
    right = np.concatenate([zero, spread], axis=2)
    first = np.stack([left, -right])
    second = np.stack([right, left])
    rows = np.stack([first, second])
    as_type = lambda a: a.astype(ml_dtypes.bfloat16)
    return as_type(pick), as_type(columns), as_type(np.swapaxes(spread, 1, 2)), as_type(rows)


def back_kernel(dims, z_ref, pick_ref, columns_ref, spread_ref, rows_ref, out_hbm, out, sems):
    beam_count, frames, stations = dims
    pairs = beam_count * frames
    z = z_ref[...].astype(BF16)
    turned = lax.dot_general(
        pick_ref[...], z, (((1,), (1,)), ((), ())), preferred_element_type=F32
    ).astype(BF16)
    row_values = []
    for kind in range(2):
        total = None
        for part in range(2):
            for pol in range(2):
                at = (part * 2 + pol) * pairs
                term = jnp.dot(
                    lax.slice(turned, (at, 0), (at + pairs, stations)),
                    rows_ref[kind, part, pol],
                    preferred_element_type=F32,
                )
                total = term if total is None else total + term
        row_values.append(total)
    column = None
    for pol in range(2):
        chosen = jnp.dot(z, columns_ref[pol], preferred_element_type=F32).astype(BF16)
        term = jnp.dot(spread_ref[pol], chosen, preferred_element_type=F32)
        column = term if column is None else column + term
    ends = []
    for b in range(beam_count):
        for f in range(frames):
            at = b * frames + f
            real = jnp.broadcast_to(
                lax.slice(column, (0, at), (2 * stations, at + 1)), (2 * stations, LANES)
            )
            imag = jnp.broadcast_to(
                lax.slice(column, (0, pairs + at), (2 * stations, pairs + at + 1)),
                (2 * stations, LANES),
            )
            one = lax.slice(row_values[0], (at, 0), (at + 1, LANES))
            two = lax.slice(row_values[1], (at, 0), (at + 1, LANES))
            out[b, f] = (real * one + imag * two).astype(BF16)
        copy = pltpu.make_async_copy(out.at[b], out_hbm.at[b], sems.at[b])
        copy.start()
        ends.append(copy)
    for copy in ends:
        copy.wait()


VMEM_SPEC = pl.BlockSpec(memory_space=pltpu.VMEM)
SMEM_SPEC = pl.BlockSpec(memory_space=pltpu.SMEM)
HBM_SPEC = pl.BlockSpec(memory_space=pltpu.HBM)


def front(sections, stations, starts, section, owner_map, taper, voltages, beam_weight_table):
    inputs = voltages.shape[1]
    taps, length = taper.shape
    frames = voltages.shape[2] // length - taps + 1
    channels = length // 2
    chunks = channels // LANES
    dims = (inputs, taps, frames, length, beam_weight_table.shape[1], sections, stations)
    return pl.pallas_call(
        functools.partial(front_kernel, dims),
        out_shape=jax.ShapeDtypeStruct((sections, channels // sections, LANES), BF16),
        in_specs=[SMEM_SPEC] + [HBM_SPEC] * 6,
        out_specs=VMEM_SPEC,
        scratch_shapes=[
            pltpu.SMEM(starts.shape, jnp.int32),
            pltpu.VMEM((1, channels), jnp.int32),
            pltpu.VMEM(taper.shape, F32),
            pltpu.VMEM((inputs, voltages.shape[2]), BF16),
            pltpu.VMEM(beam_weight_table.shape[1:], BF16),
            pltpu.VMEM((chunks, length, 2 * LANES), BF16),
            pltpu.VMEM((frames * inputs, length), BF16),
            pltpu.VMEM((beam_weight_table.shape[1], 2 * inputs, channels), F32),
            pltpu.VMEM((2, 2, frames, 2 * inputs, LANES), F32),
            pltpu.VMEM((LANES, channels), F32),
            pltpu.SemaphoreType.DMA((4 + inputs // 16 + chunks,)),
        ],
        compiler_params=pltpu.CompilerParams(vmem_limit_bytes=16 << 20),
        name="front",
    )(
        section,
        *[
            pltpu.with_memory_space_constraint(array, pltpu.HBM)
            for array in (
                starts, owner_map.reshape(1, channels), taper, voltages, beam_weight_table,
                jnp.asarray(dft_table(length)),
            )
        ],
    )


def back(beam_count, frames, z):
    stations = z.shape[0]
    shape = (beam_count, frames, 2 * stations, 4 * stations)
    matrices = [jnp.asarray(m) for m in selectors(beam_count, frames, stations)]
    return pl.pallas_call(
        functools.partial(back_kernel, (beam_count, frames, stations)),
        out_shape=jax.ShapeDtypeStruct(shape, BF16),
        in_specs=[VMEM_SPEC] * 5,
        out_specs=HBM_SPEC,
        scratch_shapes=[pltpu.VMEM(shape, BF16), pltpu.SemaphoreType.DMA((beam_count,))],
        compiler_params=pltpu.CompilerParams(vmem_limit_bytes=16 << 20),
        name="back",
    )(z, *matrices)


def local(voltages, taper, beam_weight_table, starts, owner_map):
    sections = lax.axis_size("section")
    stations = lax.axis_size("station")
    section = lax.axis_index("section").astype(jnp.int32).reshape(1)
    partial = front(
        sections, stations, starts, section, owner_map, taper, voltages, beam_weight_table
    )
    arrived = lax.all_to_all(partial, "section", split_axis=0, concat_axis=0, tiled=True)
    complete = jnp.sum(arrived.astype(F32), axis=0)
    z = lax.all_to_all(
        complete.reshape(stations, 1, LANES), "station", split_axis=0, concat_axis=0, tiled=True
    ).reshape(stations, LANES)
    beam_count = beam_weight_table.shape[1]
    frames = voltages.shape[2] // taper.shape[1] - taper.shape[0] + 1
    visible = back(beam_count, frames, z)
    return visible.reshape(1, 1, 1, *visible.shape)


def solution(mesh):
    placed = (
        P("station", "section", None),
        P(),
        P("station", None, "section", None, None),
        P(),
        P(),
    )
    return jax.shard_map(
        local,
        mesh=mesh,
        in_specs=placed,
        out_specs=P("section", "station", None, None, None, None, None),
        check_vma=False,
    )
```

```python
import functools
import math

import jax
import jax.numpy as jnp
import ml_dtypes
import numpy as np
from jax import lax
from jax.experimental import pallas as pl
from jax.experimental.pallas import tpu as pltpu
from jax.sharding import PartitionSpec as P

LANES = 128
F32 = jnp.float32
BF16 = jnp.bfloat16


def dft_table(length):
    half = length // 2
    n = np.arange(length, dtype=np.int32)[:, None]
    k = np.arange(half, dtype=np.int32)[None, :]
    phase = (n * k % length).astype(np.float32) * np.float32(2.0 * math.pi / length)
    factor = np.float32(1.0 / math.sqrt(length))
    real = (np.cos(phase) * factor).reshape(length, half // LANES, LANES)
    imag = (-np.sin(phase) * factor).reshape(length, half // LANES, LANES)
    return np.concatenate([real, imag], axis=2).reshape(length, length).astype(ml_dtypes.bfloat16)


def front_kernel(
    dims, section_ref, starts_hbm, owner_hbm, taper_hbm, volts_hbm, weights_hbm, table_hbm,
    out_ref, starts, owner, taper, volts, weights, table, rows, gain, mixed, beams, turned, sems,
):
    inputs, taps, frames, length, beam_count, sections, stations = dims
    channels = length // 2
    chunks = channels // LANES
    block = channels // sections
    half = 16
    parts = inputs // half
    starts_copy = pltpu.make_async_copy(starts_hbm, starts, sems.at[0])
    owner_copy = pltpu.make_async_copy(owner_hbm, owner, sems.at[1])
    taper_copy = pltpu.make_async_copy(taper_hbm, taper, sems.at[2])
    weight_copy = pltpu.make_async_copy(weights_hbm.at[0], weights, sems.at[3])
    volt_copies = [
        pltpu.make_async_copy(
            volts_hbm.at[0, pl.ds(i * half, half)], volts.at[pl.ds(i * half, half)], sems.at[4 + i]
        )
        for i in range(parts)
    ]
    table_copies = [
        pltpu.make_async_copy(
            table_hbm.at[:, pl.ds(c * 2 * LANES, 2 * LANES)], table.at[c], sems.at[4 + parts + c]
        )
        for c in range(chunks)
    ]
    copies = [taper_copy, *volt_copies, weight_copy, *table_copies]
    for copy in copies + [starts_copy, owner_copy]:
        copy.start()

    taper_copy.wait()
    for i in range(parts):
        volt_copies[i].wait()
        for c in range(length // LANES):
            at = c * LANES
            gains = [
                jnp.broadcast_to(taper[pl.ds(t, 1), pl.ds(at, LANES)], (half, LANES))
                for t in range(taps)
            ]
            sums = [None] * frames
            for g in range(frames + taps - 1):
                value = volts[pl.ds(i * half, half), pl.ds(g * length + at, LANES)].astype(F32)
                for f in range(frames):
                    t = g - f
                    if 0 <= t < taps:
                        term = gains[t] * value
                        sums[f] = term if sums[f] is None else sums[f] + term
            for f in range(frames):
                rows[pl.ds(f * inputs + i * half, half), pl.ds(at, LANES)] = sums[f].astype(BF16)

    starts_copy.wait()
    section = section_ref[0]
    keep = [
        jnp.where(((section - starts[b] + sections) & (sections - 1)) < sections // 2, 1.0, 0.0)
        for b in range(beam_count)
    ]
    row = lax.broadcasted_iota(jnp.int32, (8, LANES), 0)
    low = row < 4
    even = (row & 1) == 0
    tiles = 2 * inputs // 8

    def spectra_of(c):
        table_copies[c].wait()
        spectra = jnp.dot(rows[...], table[c], preferred_element_type=F32)
        for f in range(frames):
            real = lax.slice(spectra, (f * inputs, 0), ((f + 1) * inputs, LANES))
            imag = lax.slice(spectra, (f * inputs, LANES), ((f + 1) * inputs, 2 * LANES))
            for at, one, two in ((0, real, -imag), (1, imag, real)):
                mixed[c % 2, at, f, pl.ds(0, inputs, stride=2), :] = one
                mixed[c % 2, at, f, pl.ds(1, inputs, stride=2), :] = two

    weight_copy.wait()
    for b in range(beam_count):
        gain[b] = weights[b].astype(F32).reshape(2 * inputs, channels)
    owner_copy.wait()
    spectra_of(0)
    per = LANES // block
    lane = lax.broadcasted_iota(jnp.int32, (1, LANES), 1)
    slot = lax.broadcasted_iota(jnp.int32, (LANES, LANES), 0)
    for c in range(chunks):
        if c + 1 < chunks:
            spectra_of(c + 1)
        for b in range(beam_count):
            gains = [gain[b, pl.ds(8 * i, 8), pl.ds(c * LANES, LANES)] for i in range(tiles)]
            for part in range(2):
                v = []
                for f in range(frames):
                    total = None
                    for i in range(tiles):
                        term = gains[i] * mixed[c % 2, part, f, pl.ds(8 * i, 8), :]
                        total = term if total is None else total + term
                    v.append(total)
                pairs = []
                for one, two in ((v[0], v[1]), (v[2], v[3])):
                    pairs.append(
                        jnp.where(low, one, two) + pltpu.roll(jnp.where(low, two, one), 4, 0)
                    )
                one = pairs[0] + pltpu.roll(pairs[0], 7, 0)
                two = pairs[1] + pltpu.roll(pairs[1], 1, 0)
                beams[c, pl.ds(b * 16 + part * 8, 8), :] = (
                    jnp.where(even, one, two) * keep[b]
                )

        owners = owner[pl.ds(0, 1), pl.ds(c * LANES, LANES)]
        pick = jnp.where(slot == (lane // block) * block + owners, 1.0, 0.0).astype(BF16)
        placed = lax.dot_general(
            pick, beams[c].astype(BF16), (((1,), (1,)), ((), ())), preferred_element_type=F32
        )
        for s in range(per):
            turned[pl.ds(c * per + s, stations, stride=sections), :] = lax.slice(
                placed, (s * block, 0), ((s + 1) * block, LANES)
            )
    out_ref[...] = turned[...].astype(BF16).reshape(stations, sections, LANES)


def turn_kernel(in_ref, out_ref, rows):
    first, second, _ = in_ref.shape
    rows[...] = in_ref[...].astype(F32).reshape(first * second, LANES)
    for i in range(second):
        out_ref[i] = rows[pl.ds(i, first, stride=second), :].astype(BF16)


def place_of(beam, frame, part, pol):
    return beam * 16 + part * 8 + (frame & 1) * 4 + pol * 2 + (frame >> 1)


def selectors(beam_count, frames, stations):
    count = beam_count * frames * 2
    group = count // 4
    pick = np.zeros((2, 2, count, LANES), np.float32)
    columns = np.zeros((4, 2, LANES, group), np.float32)
    for b in range(beam_count):
        for f in range(frames):
            for part in range(2):
                at = (b * frames + f) * 2 + part
                for pol in range(2):
                    j = place_of(b, f, part, pol)
                    pick[0, pol, at, j] = 1
                    pick[1, pol, at, place_of(b, f, 1 - part, pol)] = 1 if part else -1
                    columns[at // group, pol, j, at % group] = 1
    spread = np.zeros((2, stations, 2 * stations), np.float32)
    for st in range(stations):
        for pol in range(2):
            spread[pol, st, 2 * st + pol] = 1
    zero = np.zeros_like(spread)
    rows = np.stack([np.concatenate([spread, zero], 2), np.concatenate([zero, spread], 2)])
    arrays = (pick.reshape(4 * count, LANES), columns, np.swapaxes(spread, 1, 2), rows)
    return [a.astype(ml_dtypes.bfloat16) for a in arrays]


def back_kernel(dims, parts_ref, pick_ref, columns_ref, spread_ref, rows_ref, out_hbm, out, sems):
    beam_count, frames, stations = dims
    count = beam_count * frames * 2
    group = count // 4
    total = parts_ref[0].astype(F32)
    for i in range(1, parts_ref.shape[0]):
        total = total + parts_ref[i].astype(F32)
    z = total.astype(BF16)
    turned = lax.dot_general(
        pick_ref[...], z, (((1,), (1,)), ((), ())), preferred_element_type=F32
    ).astype(BF16)
    right = None
    for side in range(2):
        for pol in range(2):
            at = (side * 2 + pol) * count
            term = jnp.dot(
                lax.slice(turned, (at, 0), (at + count, stations)), rows_ref[side, pol],
                preferred_element_type=F32,
            )
            right = term if right is None else right + term
    pair = lax.broadcasted_iota(jnp.int32, (group, LANES), 0) // 2
    ends = []
    for g in range(4):
        left = None
        for pol in range(2):
            chosen = jnp.dot(z, columns_ref[g, pol], preferred_element_type=F32).astype(BF16)
            term = jnp.dot(spread_ref[pol], chosen, preferred_element_type=F32)
            left = term if left is None else left + term
        left = left.astype(BF16)
        mine = lax.slice(right, (g * group, 0), ((g + 1) * group, LANES))
        spaced = jnp.concatenate(
            [jnp.where(pair == i, mine, 0.0).astype(BF16) for i in range(group // 2)], axis=1
        )
        product = jnp.dot(left, spaced, preferred_element_type=F32).astype(BF16)
        for i in range(group // 2):
            b, f = divmod(g * (group // 2) + i, frames)
            out[b, f] = lax.slice(product, (0, i * LANES), (2 * stations, (i + 1) * LANES))
            if f == frames - 1:
                copy = pltpu.make_async_copy(out.at[b], out_hbm.at[b], sems.at[b])
                copy.start()
                ends.append(copy)
    for copy in ends:
        copy.wait()


VMEM_SPEC = pl.BlockSpec(memory_space=pltpu.VMEM)
SMEM_SPEC = pl.BlockSpec(memory_space=pltpu.SMEM)
HBM_SPEC = pl.BlockSpec(memory_space=pltpu.HBM)


def front(sections, stations, starts, section, owner_map, taper, voltages, beam_weight_table):
    inputs = voltages.shape[1]
    taps, length = taper.shape
    frames = voltages.shape[2] // length - taps + 1
    channels = length // 2
    chunks = channels // LANES
    dims = (inputs, taps, frames, length, beam_weight_table.shape[1], sections, stations)
    return pl.pallas_call(
        functools.partial(front_kernel, dims),
        out_shape=jax.ShapeDtypeStruct((channels // sections, sections, LANES), BF16),
        in_specs=[SMEM_SPEC] + [HBM_SPEC] * 6,
        out_specs=VMEM_SPEC,
        scratch_shapes=[
            pltpu.SMEM(starts.shape, jnp.int32),
            pltpu.VMEM((1, channels), jnp.int32),
            pltpu.VMEM(taper.shape, F32),
            pltpu.VMEM((inputs, voltages.shape[2]), BF16),
            pltpu.VMEM(beam_weight_table.shape[1:], BF16),
            pltpu.VMEM((chunks, length, 2 * LANES), BF16),
            pltpu.VMEM((frames * inputs, length), BF16),
            pltpu.VMEM((beam_weight_table.shape[1], 2 * inputs, channels), F32),
            pltpu.VMEM((2, 2, frames, 2 * inputs, LANES), F32),
            pltpu.VMEM((chunks, LANES, LANES), F32),
            pltpu.VMEM((channels, LANES), F32),
            pltpu.SemaphoreType.DMA((4 + inputs // 16 + chunks,)),
        ],
        compiler_params=pltpu.CompilerParams(vmem_limit_bytes=16 << 20),
        name="front",
    )(
        section,
        *[
            pltpu.with_memory_space_constraint(array, pltpu.HBM)
            for array in (
                starts, owner_map.reshape(1, channels), taper, voltages, beam_weight_table,
                jnp.asarray(dft_table(length)),
            )
        ],
    )


def turn(array):
    first, second, _ = array.shape
    return pl.pallas_call(
        turn_kernel,
        out_shape=jax.ShapeDtypeStruct((second, first, LANES), BF16),
        in_specs=[VMEM_SPEC],
        out_specs=VMEM_SPEC,
        scratch_shapes=[pltpu.VMEM((first * second, LANES), F32)],
        compiler_params=pltpu.CompilerParams(vmem_limit_bytes=4 << 20),
        name="turn",
    )(array)


def back(beam_count, frames, parts):
    stations = parts.shape[1]
    shape = (beam_count, frames, 2 * stations, 4 * stations)
    matrices = [jnp.asarray(m) for m in selectors(beam_count, frames, stations)]
    return pl.pallas_call(
        functools.partial(back_kernel, (beam_count, frames, stations)),
        out_shape=jax.ShapeDtypeStruct(shape, BF16),
        in_specs=[VMEM_SPEC] * 5,
        out_specs=HBM_SPEC,
        scratch_shapes=[pltpu.VMEM(shape, BF16), pltpu.SemaphoreType.DMA((beam_count,))],
        compiler_params=pltpu.CompilerParams(vmem_limit_bytes=16 << 20),
        name="back",
    )(parts, *matrices)


def local(voltages, taper, beam_weight_table, starts, owner_map):
    sections = lax.axis_size("section")
    stations = lax.axis_size("station")
    section = lax.axis_index("section").astype(jnp.int32).reshape(1)
    parts = front(
        sections, stations, starts, section, owner_map, taper, voltages, beam_weight_table
    )
    parts = lax.all_to_all(parts, "station", split_axis=0, concat_axis=0, tiled=True)
    parts = lax.all_to_all(turn(parts), "section", split_axis=0, concat_axis=0, tiled=True)
    beam_count = beam_weight_table.shape[1]
    frames = voltages.shape[2] // taper.shape[1] - taper.shape[0] + 1
    visible = back(beam_count, frames, parts)
    return visible.reshape(1, 1, 1, *visible.shape)


def solution(mesh):
    placed = (
        P("station", "section", None),
        P(),
        P("station", None, "section", None, None),
        P(),
        P(),
    )
    return jax.shard_map(
        local,
        mesh=mesh,
        in_specs=placed,
        out_specs=P("section", "station", None, None, None, None, None),
        check_vma=False,
    )
```

```python
import functools
import math

import jax
import jax.numpy as jnp
import ml_dtypes
import numpy as np
from jax import lax
from jax.experimental import pallas as pl
from jax.experimental.pallas import tpu as pltpu
from jax.sharding import PartitionSpec as P

LANES = 128
DEPTH = 256
F32 = jnp.float32
BF16 = jnp.bfloat16


def dft_table(length):
    count = length // 4
    n = np.arange(length, dtype=np.int32)[:, None]
    k = np.arange(count, dtype=np.int32)[None, :]
    phase = (n * k % length).astype(np.float32) * np.float32(2.0 * math.pi / length)
    factor = np.float32(1.0 / math.sqrt(length))
    real = (np.cos(phase) * factor).reshape(length, count // LANES, LANES)
    imag = (-np.sin(phase) * factor).reshape(length, count // LANES, LANES)
    table = np.concatenate([real, imag], axis=2).reshape(length // DEPTH, DEPTH, 2 * count)
    return table.astype(ml_dtypes.bfloat16)


def front_kernel(
    dims, section_ref, starts_hbm, owner_hbm, taper_hbm, volts_hbm, weights_hbm, table_hbm,
    out_ref, starts, owner, taper, volts, weights, table, gain, beams, turned, sems, *rest,
):
    inputs, taps, frames, length, beam_count, sections, stations = dims
    channels = length // 2
    chunks = channels // LANES
    block = channels // sections
    depths = length // DEPTH
    mixed, rows = rest[:chunks], rest[chunks:]
    half = 16
    parts = inputs // half
    starts_copy = pltpu.make_async_copy(starts_hbm, starts, sems.at[0])
    owner_copy = pltpu.make_async_copy(owner_hbm, owner, sems.at[1])
    taper_copy = pltpu.make_async_copy(taper_hbm, taper, sems.at[2])
    weight_copy = pltpu.make_async_copy(weights_hbm.at[0], weights, sems.at[3])
    volt_copies = [
        pltpu.make_async_copy(
            volts_hbm.at[0, pl.ds(i * half, half)], volts.at[pl.ds(i * half, half)], sems.at[4 + i]
        )
        for i in range(parts)
    ]
    table_copies = [
        pltpu.make_async_copy(
            table_hbm.at[c], table.at[c], sems.at[4 + parts + c]
        )
        for c in range(depths)
    ]
    small = [taper_copy, starts_copy, owner_copy]
    for copy in small + volt_copies + table_copies + [weight_copy]:
        copy.start()

    turns = lax.broadcasted_iota(jnp.int32, (half, LANES), 1) & 3
    signs = [
        jnp.where(turns == i, 1.0, jnp.where(turns == i + 2, -1.0, 0.0)).astype(BF16)
        for i in range(2)
    ]
    def filter_of(d, i):
        for c in range(DEPTH // LANES):
            at = d * DEPTH + c * LANES
            gains = [
                jnp.broadcast_to(taper[pl.ds(t, 1), pl.ds(at, LANES)], (half, LANES))
                for t in range(taps)
            ]
            sums = [None] * frames
            for g in range(frames + taps - 1):
                value = volts[pl.ds(i * half, half), pl.ds(g * length + at, LANES)].astype(F32)
                for f in range(frames):
                    t = g - f
                    if 0 <= t < taps:
                        term = gains[t] * value
                        sums[f] = term if sums[f] is None else sums[f] + term
            for f in range(frames):
                plain = sums[f].astype(BF16)
                for r, value in enumerate((plain, plain * signs[0], plain * signs[1])):
                    place = (r * frames + f) * inputs + i * half
                    rows[d][pl.ds(place, half), pl.ds(c * LANES, LANES)] = value

    for copy in small:
        copy.wait()
    for i in range(parts):
        volt_copies[i].wait()
        filter_of(0, i)
    spectra = None
    for d in range(depths):
        table_copies[d].wait()
        if d == depths - 1:
            weight_copy.wait()
        term = jnp.dot(rows[d][...], table[d], preferred_element_type=F32)
        spectra = term if spectra is None else spectra + term
        if d + 1 < depths:
            for i in range(parts):
                filter_of(d + 1, i)
    for b in range(beam_count):
        gain[b] = weights[b].astype(F32).reshape(2 * inputs, channels)

    section = section_ref[0]
    keep = [
        jnp.where(((section - starts[b] + sections) & (sections - 1)) < sections // 2, 1.0, 0.0)
        for b in range(beam_count)
    ]
    row = lax.broadcasted_iota(jnp.int32, (8, LANES), 0)
    low = row < 4
    even = (row & 1) == 0
    tiles = 2 * inputs // 8

    def keep_spectra(c, f, real, imag):
        for part, one, two in ((0, real, -imag), (1, imag, real)):
            mixed[c][part, f, pl.ds(0, inputs, stride=2), :] = one
            mixed[c][part, f, pl.ds(1, inputs, stride=2), :] = two

    def spectra_of(c):
        def take(r, f, part):
            at = (r * frames + f) * inputs
            lane = (2 * c + part) * LANES
            return lax.slice(spectra, (at, lane), (at + inputs, lane + LANES))

        for f in range(frames):
            keep_spectra(c, f, take(0, f, 0), take(0, f, 1))
            keep_spectra(
                c + chunks // 2, f,
                take(1, f, 0) + take(2, f, 1), take(1, f, 1) - take(2, f, 0),
            )

    for c in range(chunks // 2):
        spectra_of(c)
    per = LANES // block
    lane = lax.broadcasted_iota(jnp.int32, (1, LANES), 1)
    slot = lax.broadcasted_iota(jnp.int32, (LANES, LANES), 0)
    for c in sorted(range(chunks), key=lambda c: c % (chunks // 2)):
        for b in range(beam_count):
            gains = [gain[b, pl.ds(8 * i, 8), pl.ds(c * LANES, LANES)] for i in range(tiles)]
            for part in range(2):
                v = []
                for f in range(frames):
                    total = None
                    for i in range(tiles):
                        term = gains[i] * mixed[c][part, f, pl.ds(8 * i, 8), :]
                        total = term if total is None else total + term
                    v.append(total)
                pairs = []
                for one, two in ((v[0], v[1]), (v[2], v[3])):
                    pairs.append(
                        jnp.where(low, one, two) + pltpu.roll(jnp.where(low, two, one), 4, 0)
                    )
                one = pairs[0] + pltpu.roll(pairs[0], 7, 0)
                two = pairs[1] + pltpu.roll(pairs[1], 1, 0)
                beams[c, pl.ds(b * 16 + part * 8, 8), :] = (
                    jnp.where(even, one, two) * keep[b]
                )

        owners = owner[pl.ds(0, 1), pl.ds(c * LANES, LANES)]
        pick = jnp.where(slot == (lane // block) * block + owners, 1.0, 0.0).astype(BF16)
        placed = lax.dot_general(
            pick, beams[c].astype(BF16), (((1,), (1,)), ((), ())), preferred_element_type=F32
        )
        for s in range(per):
            turned[pl.ds(c * per + s, stations, stride=sections), :] = lax.slice(
                placed, (s * block, 0), ((s + 1) * block, LANES)
            )
    out_ref[...] = turned[...].astype(BF16).reshape(stations, sections, LANES)


def turn_kernel(in_ref, out_ref, rows):
    first, second, _ = in_ref.shape
    rows[...] = in_ref[...].astype(F32).reshape(first * second, LANES)
    for i in range(second):
        out_ref[i] = rows[pl.ds(i, first, stride=second), :].astype(BF16)


def place_of(beam, frame, part, pol):
    return beam * 16 + part * 8 + (frame & 1) * 4 + pol * 2 + (frame >> 1)


def selectors(beam_count, frames, stations):
    count = beam_count * frames * 2
    pick = np.zeros((2, 2, count, LANES), np.float32)
    columns = np.zeros((2, LANES, count), np.float32)
    for b in range(beam_count):
        for f in range(frames):
            for part in range(2):
                at = (b * frames + f) * 2 + part
                for pol in range(2):
                    j = place_of(b, f, part, pol)
                    pick[0, pol, at, j] = 1
                    pick[1, pol, at, place_of(b, f, 1 - part, pol)] = 1 if part else -1
                    columns[pol, j, at] = 1
    spread = np.zeros((2, stations, 2 * stations), np.float32)
    for st in range(stations):
        for pol in range(2):
            spread[pol, st, 2 * st + pol] = 1
    zero = np.zeros_like(spread)
    rows = np.stack([np.concatenate([spread, zero], 2), np.concatenate([zero, spread], 2)])
    arrays = (pick.reshape(4 * count, LANES), columns, np.swapaxes(spread, 1, 2), rows)
    return [a.astype(ml_dtypes.bfloat16) for a in arrays]


def back_kernel(dims, parts_ref, pick_ref, columns_ref, spread_ref, rows_ref, out_hbm, out, sems):
    beam_count, frames, stations = dims
    count = beam_count * frames * 2
    total = parts_ref[0].astype(F32)
    for i in range(1, parts_ref.shape[0]):
        total = total + parts_ref[i].astype(F32)
    z = total.astype(BF16)
    turned = lax.dot_general(
        pick_ref[...], z, (((1,), (1,)), ((), ())), preferred_element_type=F32
    ).astype(BF16)
    right = None
    for side in range(2):
        for pol in range(2):
            at = (side * 2 + pol) * count
            term = jnp.dot(
                lax.slice(turned, (at, 0), (at + count, stations)), rows_ref[side, pol],
                preferred_element_type=F32,
            )
            right = term if right is None else right + term
    left = None
    for pol in range(2):
        chosen = jnp.dot(z, columns_ref[pol], preferred_element_type=F32).astype(BF16)
        term = jnp.dot(spread_ref[pol], chosen, preferred_element_type=F32)
        left = term if left is None else left + term
    upper = lax.broadcasted_iota(jnp.int32, (count, LANES), 0) < count // 2
    held = jnp.concatenate(
        [jnp.where(upper, right, 0.0), jnp.where(upper, 0.0, right)], axis=1
    ).astype(BF16)
    pair = (lax.broadcasted_iota(jnp.int32, left.shape, 1) & (count // 2 - 1)) // 2
    ends = []
    for b in range(beam_count // 2):
        streamed = jnp.concatenate(
            [jnp.where(pair == b * frames + f, left, 0.0).astype(BF16) for f in range(frames)],
            axis=0,
        )
        product = jnp.dot(streamed, held, preferred_element_type=F32).astype(BF16)
        for side in range(2):
            at = b + side * (beam_count // 2)
            for f in range(frames):
                out[at, f] = lax.slice(
                    product, (f * 2 * stations, side * LANES),
                    ((f + 1) * 2 * stations, (side + 1) * LANES),
                )
            copy = pltpu.make_async_copy(out.at[at], out_hbm.at[at], sems.at[at])
            copy.start()
            ends.append(copy)
    for copy in ends:
        copy.wait()


VMEM_SPEC = pl.BlockSpec(memory_space=pltpu.VMEM)
SMEM_SPEC = pl.BlockSpec(memory_space=pltpu.SMEM)
HBM_SPEC = pl.BlockSpec(memory_space=pltpu.HBM)


def front(sections, stations, starts, section, owner_map, taper, voltages, beam_weight_table):
    inputs = voltages.shape[1]
    taps, length = taper.shape
    frames = voltages.shape[2] // length - taps + 1
    channels = length // 2
    chunks = channels // LANES
    dims = (inputs, taps, frames, length, beam_weight_table.shape[1], sections, stations)
    return pl.pallas_call(
        functools.partial(front_kernel, dims),
        out_shape=jax.ShapeDtypeStruct((channels // sections, sections, LANES), BF16),
        in_specs=[SMEM_SPEC] + [HBM_SPEC] * 6,
        out_specs=VMEM_SPEC,
        scratch_shapes=[
            pltpu.SMEM(starts.shape, jnp.int32),
            pltpu.VMEM((1, channels), jnp.int32),
            pltpu.VMEM(taper.shape, F32),
            pltpu.VMEM((inputs, voltages.shape[2]), BF16),
            pltpu.VMEM(beam_weight_table.shape[1:], BF16),
            pltpu.VMEM((length // DEPTH, DEPTH, channels), BF16),
            pltpu.VMEM((beam_weight_table.shape[1], 2 * inputs, channels), F32),
            pltpu.VMEM((chunks, LANES, LANES), F32),
            pltpu.VMEM((channels, LANES), F32),
            pltpu.SemaphoreType.DMA((4 + inputs // 16 + length // DEPTH,)),
            *[pltpu.VMEM((2, frames, 2 * inputs, LANES), F32)] * chunks,
            *[pltpu.VMEM((3 * frames * inputs, DEPTH), BF16)] * (length // DEPTH),
        ],
        compiler_params=pltpu.CompilerParams(vmem_limit_bytes=16 << 20),
        name="front",
    )(
        section,
        *[
            pltpu.with_memory_space_constraint(array, pltpu.HBM)
            for array in (
                starts, owner_map.reshape(1, channels), taper, voltages, beam_weight_table,
                jnp.asarray(dft_table(length)),
            )
        ],
    )


def turn(array):
    first, second, _ = array.shape
    return pl.pallas_call(
        turn_kernel,
        out_shape=jax.ShapeDtypeStruct((second, first, LANES), BF16),
        in_specs=[VMEM_SPEC],
        out_specs=VMEM_SPEC,
        scratch_shapes=[pltpu.VMEM((first * second, LANES), F32)],
        compiler_params=pltpu.CompilerParams(vmem_limit_bytes=4 << 20),
        name="turn",
    )(array)


def back(beam_count, frames, parts):
    stations = parts.shape[1]
    shape = (beam_count, frames, 2 * stations, 4 * stations)
    matrices = [jnp.asarray(m) for m in selectors(beam_count, frames, stations)]
    return pl.pallas_call(
        functools.partial(back_kernel, (beam_count, frames, stations)),
        out_shape=jax.ShapeDtypeStruct(shape, BF16),
        in_specs=[VMEM_SPEC] * 5,
        out_specs=HBM_SPEC,
        scratch_shapes=[pltpu.VMEM(shape, BF16), pltpu.SemaphoreType.DMA((beam_count,))],
        compiler_params=pltpu.CompilerParams(vmem_limit_bytes=16 << 20),
        name="back",
    )(parts, *matrices)


def local(voltages, taper, beam_weight_table, starts, owner_map):
    sections = lax.axis_size("section")
    stations = lax.axis_size("station")
    section = lax.axis_index("section").astype(jnp.int32).reshape(1)
    parts = front(
        sections, stations, starts, section, owner_map, taper, voltages, beam_weight_table
    )
    parts = lax.all_to_all(parts, "station", split_axis=0, concat_axis=0, tiled=True)
    parts = lax.all_to_all(turn(parts), "section", split_axis=0, concat_axis=0, tiled=True)
    beam_count = beam_weight_table.shape[1]
    frames = voltages.shape[2] // taper.shape[1] - taper.shape[0] + 1
    visible = back(beam_count, frames, parts)
    return visible.reshape(1, 1, 1, *visible.shape)


def solution(mesh):
    placed = (
        P("station", "section", None),
        P(),
        P("station", None, "section", None, None),
        P(),
        P(),
    )
    return jax.shard_map(
        local,
        mesh=mesh,
        in_specs=placed,
        out_specs=P("section", "station", None, None, None, None, None),
        check_vma=False,
    )
```

```python
import functools
import math

import jax
import jax.numpy as jnp
import ml_dtypes
import numpy as np
from jax import lax
from jax.experimental import pallas as pl
from jax.experimental.pallas import tpu as pltpu
from jax.sharding import PartitionSpec as P

LANES = 128
DEPTH = 256
LEAD_SECTION = 10
LEAD_STATION = 20
F32 = jnp.float32
BF16 = jnp.bfloat16


def turned_order(count, lead):
    return [(lead + i) % count for i in range(count)]


def dft_table(length):
    count = length // 4
    n = np.arange(length, dtype=np.int32)[:, None]
    k = np.arange(count, dtype=np.int32)[None, :]
    phase = (n * k % length).astype(np.float32) * np.float32(2.0 * math.pi / length)
    factor = np.float32(1.0 / math.sqrt(length))
    real = (np.cos(phase) * factor).reshape(length, count // LANES, LANES)
    imag = (-np.sin(phase) * factor).reshape(length, count // LANES, LANES)
    table = np.concatenate([real, imag], axis=2).reshape(length // DEPTH, DEPTH, 2 * count)
    return table.astype(ml_dtypes.bfloat16)


def front_kernel(
    dims, section_ref, starts_hbm, owner_hbm, taper_hbm, volts_hbm, weights_hbm, table_hbm,
    out_ref, starts, owner, taper, volts, weights, table, gain, beams, turned, sems, *rest,
):
    inputs, taps, frames, length, beam_count, sections, stations = dims
    channels = length // 2
    chunks = channels // LANES
    block = channels // sections
    depths = length // DEPTH
    mixed, rows = rest[:chunks], rest[chunks:]
    half = 16
    parts = inputs // half
    starts_copy = pltpu.make_async_copy(starts_hbm, starts, sems.at[0])
    owner_copy = pltpu.make_async_copy(owner_hbm, owner, sems.at[1])
    taper_copy = pltpu.make_async_copy(taper_hbm, taper, sems.at[2])
    weight_copy = pltpu.make_async_copy(weights_hbm.at[0], weights, sems.at[3])
    volt_copies = [
        pltpu.make_async_copy(
            volts_hbm.at[0, pl.ds(i * half, half)], volts.at[pl.ds(i * half, half)], sems.at[4 + i]
        )
        for i in range(parts)
    ]
    table_copies = [
        pltpu.make_async_copy(
            table_hbm.at[c], table.at[c], sems.at[4 + parts + c]
        )
        for c in range(depths)
    ]
    small = [taper_copy, starts_copy, owner_copy]
    for copy in small + volt_copies + table_copies + [weight_copy]:
        copy.start()

    turns = lax.broadcasted_iota(jnp.int32, (half, LANES), 1) & 3
    signs = [
        jnp.where(turns == i, 1.0, jnp.where(turns == i + 2, -1.0, 0.0)).astype(BF16)
        for i in range(2)
    ]
    def filter_of(d, i):
        for c in range(DEPTH // LANES):
            at = d * DEPTH + c * LANES
            gains = [
                jnp.broadcast_to(taper[pl.ds(t, 1), pl.ds(at, LANES)], (half, LANES))
                for t in range(taps)
            ]
            sums = [None] * frames
            for g in range(frames + taps - 1):
                value = volts[pl.ds(i * half, half), pl.ds(g * length + at, LANES)].astype(F32)
                for f in range(frames):
                    t = g - f
                    if 0 <= t < taps:
                        term = gains[t] * value
                        sums[f] = term if sums[f] is None else sums[f] + term
            for f in range(frames):
                plain = sums[f].astype(BF16)
                for r, value in enumerate((plain, plain * signs[0], plain * signs[1])):
                    place = (r * frames + f) * inputs + i * half
                    rows[d][pl.ds(place, half), pl.ds(c * LANES, LANES)] = value

    for copy in small:
        copy.wait()
    for i in range(parts):
        volt_copies[i].wait()
        filter_of(0, i)
    spectra = None
    for d in range(depths):
        table_copies[d].wait()
        if d == depths - 1:
            weight_copy.wait()
        term = jnp.dot(rows[d][...], table[d], preferred_element_type=F32)
        spectra = term if spectra is None else spectra + term
        if d + 1 < depths:
            for i in range(parts):
                filter_of(d + 1, i)
    for b in range(beam_count):
        gain[b] = weights[b].astype(F32).reshape(2 * inputs, channels)

    section = section_ref[0]
    keep = [
        jnp.where(((section - starts[b] + sections) & (sections - 1)) < sections // 2, 1.0, 0.0)
        for b in range(beam_count)
    ]
    row = lax.broadcasted_iota(jnp.int32, (8, LANES), 0)
    low = row < 4
    even = (row & 1) == 0
    tiles = 2 * inputs // 8

    def keep_spectra(c, f, real, imag):
        for part, one, two in ((0, real, -imag), (1, imag, real)):
            mixed[c][part, f, pl.ds(0, inputs, stride=2), :] = one
            mixed[c][part, f, pl.ds(1, inputs, stride=2), :] = two

    def spectra_of(c):
        def take(r, f, part):
            at = (r * frames + f) * inputs
            lane = (2 * c + part) * LANES
            return lax.slice(spectra, (at, lane), (at + inputs, lane + LANES))

        for f in range(frames):
            keep_spectra(c, f, take(0, f, 0), take(0, f, 1))
            keep_spectra(
                c + chunks // 2, f,
                take(1, f, 0) + take(2, f, 1), take(1, f, 1) - take(2, f, 0),
            )

    for c in range(chunks // 2):
        spectra_of(c)
    per = LANES // block
    lane = lax.broadcasted_iota(jnp.int32, (1, LANES), 1)
    slot = lax.broadcasted_iota(jnp.int32, (LANES, LANES), 0)
    for c in sorted(range(chunks), key=lambda c: c % (chunks // 2)):
        for b in range(beam_count):
            gains = [gain[b, pl.ds(8 * i, 8), pl.ds(c * LANES, LANES)] for i in range(tiles)]
            for part in range(2):
                v = []
                for f in range(frames):
                    total = None
                    for i in range(tiles):
                        term = gains[i] * mixed[c][part, f, pl.ds(8 * i, 8), :]
                        total = term if total is None else total + term
                    v.append(total)
                pairs = []
                for one, two in ((v[0], v[1]), (v[2], v[3])):
                    pairs.append(
                        jnp.where(low, one, two) + pltpu.roll(jnp.where(low, two, one), 4, 0)
                    )
                one = pairs[0] + pltpu.roll(pairs[0], 7, 0)
                two = pairs[1] + pltpu.roll(pairs[1], 1, 0)
                beams[c, pl.ds(b * 16 + part * 8, 8), :] = (
                    jnp.where(even, one, two) * keep[b]
                )

        owners = owner[pl.ds(0, 1), pl.ds(c * LANES, LANES)]
        spot = (owners + (stations - LEAD_STATION % stations)) & (stations - 1)
        pick = jnp.where(slot == (lane // block) * block + spot, 1.0, 0.0).astype(BF16)
        placed = lax.dot_general(
            pick, beams[c].astype(BF16), (((1,), (1,)), ((), ())), preferred_element_type=F32
        )
        for s in range(per):
            turned[pl.ds(c * per + s, stations, stride=sections), :] = lax.slice(
                placed, (s * block, 0), ((s + 1) * block, LANES)
            )
    out_ref[...] = turned[...].astype(BF16).reshape(stations, sections, LANES)


def turn_kernel(in_ref, out_ref, rows):
    first, second, _ = in_ref.shape
    rows[...] = in_ref[...].astype(F32).reshape(first * second, LANES)
    for i, section in enumerate(turned_order(second, LEAD_SECTION)):
        out_ref[i] = rows[pl.ds(section, first, stride=second), :].astype(BF16)


def place_of(beam, frame, part, pol):
    return beam * 16 + part * 8 + (frame & 1) * 4 + pol * 2 + (frame >> 1)


def selectors(beam_count, frames, stations):
    count = beam_count * frames * 2
    pick = np.zeros((2, 2, count, LANES), np.float32)
    columns = np.zeros((2, LANES, count), np.float32)
    for b in range(beam_count):
        for f in range(frames):
            for part in range(2):
                at = (b * frames + f) * 2 + part
                for pol in range(2):
                    j = place_of(b, f, part, pol)
                    pick[0, pol, at, j] = 1
                    pick[1, pol, at, place_of(b, f, 1 - part, pol)] = 1 if part else -1
                    columns[pol, j, at] = 1
    spread = np.zeros((2, stations, 2 * stations), np.float32)
    for i, station in enumerate(turned_order(stations, LEAD_STATION)):
        for pol in range(2):
            spread[pol, i, 2 * station + pol] = 1
    zero = np.zeros_like(spread)
    rows = np.stack([np.concatenate([spread, zero], 2), np.concatenate([zero, spread], 2)])
    arrays = (pick.reshape(4 * count, LANES), columns, np.swapaxes(spread, 1, 2), rows)
    return [a.astype(ml_dtypes.bfloat16) for a in arrays]


def back_kernel(dims, parts_ref, pick_ref, columns_ref, spread_ref, rows_ref, out_hbm, out, sems):
    beam_count, frames, stations = dims
    count = beam_count * frames * 2
    total = parts_ref[0].astype(F32)
    for i in range(1, parts_ref.shape[0]):
        total = total + parts_ref[i].astype(F32)
    z = total.astype(BF16)
    turned = lax.dot_general(
        pick_ref[...], z, (((1,), (1,)), ((), ())), preferred_element_type=F32
    ).astype(BF16)
    right = None
    for side in range(2):
        for pol in range(2):
            at = (side * 2 + pol) * count
            term = jnp.dot(
                lax.slice(turned, (at, 0), (at + count, stations)), rows_ref[side, pol],
                preferred_element_type=F32,
            )
            right = term if right is None else right + term
    left = None
    for pol in range(2):
        chosen = jnp.dot(z, columns_ref[pol], preferred_element_type=F32).astype(BF16)
        term = jnp.dot(spread_ref[pol], chosen, preferred_element_type=F32)
        left = term if left is None else left + term
    upper = lax.broadcasted_iota(jnp.int32, (count, LANES), 0) < count // 2
    held = jnp.concatenate(
        [jnp.where(upper, right, 0.0), jnp.where(upper, 0.0, right)], axis=1
    ).astype(BF16)
    pair = (lax.broadcasted_iota(jnp.int32, left.shape, 1) & (count // 2 - 1)) // 2
    ends = []
    for b in range(beam_count // 2):
        streamed = jnp.concatenate(
            [jnp.where(pair == b * frames + f, left, 0.0).astype(BF16) for f in range(frames)],
            axis=0,
        )
        product = jnp.dot(streamed, held, preferred_element_type=F32).astype(BF16)
        for side in range(2):
            at = b + side * (beam_count // 2)
            for f in range(frames):
                out[at, f] = lax.slice(
                    product, (f * 2 * stations, side * LANES),
                    ((f + 1) * 2 * stations, (side + 1) * LANES),
                )
            copy = pltpu.make_async_copy(out.at[at], out_hbm.at[at], sems.at[at])
            copy.start()
            ends.append(copy)
    for copy in ends:
        copy.wait()


VMEM_SPEC = pl.BlockSpec(memory_space=pltpu.VMEM)
SMEM_SPEC = pl.BlockSpec(memory_space=pltpu.SMEM)
HBM_SPEC = pl.BlockSpec(memory_space=pltpu.HBM)


def front(sections, stations, starts, section, owner_map, taper, voltages, beam_weight_table):
    inputs = voltages.shape[1]
    taps, length = taper.shape
    frames = voltages.shape[2] // length - taps + 1
    channels = length // 2
    chunks = channels // LANES
    dims = (inputs, taps, frames, length, beam_weight_table.shape[1], sections, stations)
    return pl.pallas_call(
        functools.partial(front_kernel, dims),
        out_shape=jax.ShapeDtypeStruct((channels // sections, sections, LANES), BF16),
        in_specs=[SMEM_SPEC] + [HBM_SPEC] * 6,
        out_specs=VMEM_SPEC,
        scratch_shapes=[
            pltpu.SMEM(starts.shape, jnp.int32),
            pltpu.VMEM((1, channels), jnp.int32),
            pltpu.VMEM(taper.shape, F32),
            pltpu.VMEM((inputs, voltages.shape[2]), BF16),
            pltpu.VMEM(beam_weight_table.shape[1:], BF16),
            pltpu.VMEM((length // DEPTH, DEPTH, channels), BF16),
            pltpu.VMEM((beam_weight_table.shape[1], 2 * inputs, channels), F32),
            pltpu.VMEM((chunks, LANES, LANES), F32),
            pltpu.VMEM((channels, LANES), F32),
            pltpu.SemaphoreType.DMA((4 + inputs // 16 + length // DEPTH,)),
            *[pltpu.VMEM((2, frames, 2 * inputs, LANES), F32)] * chunks,
            *[pltpu.VMEM((3 * frames * inputs, DEPTH), BF16)] * (length // DEPTH),
        ],
        compiler_params=pltpu.CompilerParams(vmem_limit_bytes=16 << 20),
        name="front",
    )(
        section,
        *[
            pltpu.with_memory_space_constraint(array, pltpu.HBM)
            for array in (
                starts, owner_map.reshape(1, channels), taper, voltages, beam_weight_table,
                jnp.asarray(dft_table(length)),
            )
        ],
    )


def turn(array):
    first, second, _ = array.shape
    return pl.pallas_call(
        turn_kernel,
        out_shape=jax.ShapeDtypeStruct((second, first, LANES), BF16),
        in_specs=[VMEM_SPEC],
        out_specs=VMEM_SPEC,
        scratch_shapes=[pltpu.VMEM((first * second, LANES), F32)],
        compiler_params=pltpu.CompilerParams(vmem_limit_bytes=4 << 20),
        name="turn",
    )(array)


def back(beam_count, frames, parts):
    stations = parts.shape[1]
    shape = (beam_count, frames, 2 * stations, 4 * stations)
    matrices = [jnp.asarray(m) for m in selectors(beam_count, frames, stations)]
    return pl.pallas_call(
        functools.partial(back_kernel, (beam_count, frames, stations)),
        out_shape=jax.ShapeDtypeStruct(shape, BF16),
        in_specs=[VMEM_SPEC] * 5,
        out_specs=HBM_SPEC,
        scratch_shapes=[pltpu.VMEM(shape, BF16), pltpu.SemaphoreType.DMA((beam_count,))],
        compiler_params=pltpu.CompilerParams(vmem_limit_bytes=16 << 20),
        name="back",
    )(parts, *matrices)


def exchange(blocks, axis, lead):
    groups = [turned_order(lax.axis_size(axis), lead)]
    return lax.all_to_all(
        blocks, axis, split_axis=0, concat_axis=0, tiled=True, axis_index_groups=groups
    )


def local(voltages, taper, beam_weight_table, starts, owner_map):
    sections = lax.axis_size("section")
    stations = lax.axis_size("station")
    section = lax.axis_index("section").astype(jnp.int32).reshape(1)
    parts = front(
        sections, stations, starts, section, owner_map, taper, voltages, beam_weight_table
    )
    parts = exchange(parts, "station", LEAD_STATION)
    parts = exchange(turn(parts), "section", LEAD_SECTION)
    beam_count = beam_weight_table.shape[1]
    frames = voltages.shape[2] // taper.shape[1] - taper.shape[0] + 1
    visible = back(beam_count, frames, parts)
    return visible.reshape(1, 1, 1, *visible.shape)


def solution(mesh):
    placed = (
        P("station", "section", None),
        P(),
        P("station", None, "section", None, None),
        P(),
        P(),
    )
    return jax.shard_map(
        local,
        mesh=mesh,
        in_specs=placed,
        out_specs=P("section", "station", None, None, None, None, None),
        check_vma=False,
    )
```

```python
import functools
import math

import jax
import jax.numpy as jnp
import ml_dtypes
import numpy as np
from jax import lax
from jax.experimental import pallas as pl
from jax.experimental.pallas import tpu as pltpu
from jax.sharding import PartitionSpec as P

LANES = 128
DEPTH = 256
LEAD_SECTION = 10
LEAD_STATION = 21
F32 = jnp.float32
BF16 = jnp.bfloat16


def turned_order(count, lead):
    return [(lead + i) % count for i in range(count)]


def dft_table(length):
    count = length // 4
    n = np.arange(length, dtype=np.int32)[:, None]
    k = np.arange(count, dtype=np.int32)[None, :]
    phase = (n * k % length).astype(np.float32) * np.float32(2.0 * math.pi / length)
    factor = np.float32(1.0 / math.sqrt(length))
    real = (np.cos(phase) * factor).reshape(length, count // LANES, LANES)
    imag = (-np.sin(phase) * factor).reshape(length, count // LANES, LANES)
    table = np.concatenate([real, imag], axis=2).reshape(length // DEPTH, DEPTH, 2 * count)
    return table.astype(ml_dtypes.bfloat16)


def front_kernel(
    dims, section_ref, starts_hbm, owner_hbm, taper_hbm, volts_hbm, weights_hbm, table_hbm,
    out_ref, starts, owner, taper, volts, weights, table, gain, beams, sems, *rest,
):
    inputs, taps, frames, length, beam_count, sections, stations = dims
    channels = length // 2
    chunks = channels // LANES
    block = channels // sections
    depths = length // DEPTH
    mixed, rows = rest[:chunks], rest[chunks:]
    half = 16
    parts = inputs // half
    starts_copy = pltpu.make_async_copy(starts_hbm, starts, sems.at[0])
    owner_copy = pltpu.make_async_copy(owner_hbm, owner, sems.at[1])
    taper_copy = pltpu.make_async_copy(taper_hbm, taper, sems.at[2])
    weight_copy = pltpu.make_async_copy(weights_hbm.at[0], weights, sems.at[3])
    volt_copies = [
        pltpu.make_async_copy(
            volts_hbm.at[0, pl.ds(i * half, half)], volts.at[pl.ds(i * half, half)], sems.at[4 + i]
        )
        for i in range(parts)
    ]
    table_copies = [
        pltpu.make_async_copy(
            table_hbm.at[c], table.at[c], sems.at[4 + parts + c]
        )
        for c in range(depths)
    ]
    small = [taper_copy, starts_copy, owner_copy]
    for copy in small + volt_copies + table_copies + [weight_copy]:
        copy.start()

    turns = lax.broadcasted_iota(jnp.int32, (half, LANES), 1) & 3
    signs = [
        jnp.where(turns == i, 1.0, jnp.where(turns == i + 2, -1.0, 0.0)).astype(BF16)
        for i in range(2)
    ]
    def filter_of(d, i):
        for c in range(DEPTH // LANES):
            at = d * DEPTH + c * LANES
            gains = [
                jnp.broadcast_to(taper[pl.ds(t, 1), pl.ds(at, LANES)], (half, LANES))
                for t in range(taps)
            ]
            sums = [None] * frames
            for g in range(frames + taps - 1):
                value = volts[pl.ds(i * half, half), pl.ds(g * length + at, LANES)].astype(F32)
                for f in range(frames):
                    t = g - f
                    if 0 <= t < taps:
                        term = gains[t] * value
                        sums[f] = term if sums[f] is None else sums[f] + term
            for f in range(frames):
                plain = sums[f].astype(BF16)
                for r, value in enumerate((plain, plain * signs[0], plain * signs[1])):
                    place = (r * frames + f) * inputs + i * half
                    rows[d][pl.ds(place, half), pl.ds(c * LANES, LANES)] = value

    for copy in small:
        copy.wait()
    for i in range(parts):
        volt_copies[i].wait()
        filter_of(0, i)
    spectra = None
    for d in range(depths):
        table_copies[d].wait()
        if d == depths - 1:
            weight_copy.wait()
        term = jnp.dot(rows[d][...], table[d], preferred_element_type=F32)
        spectra = term if spectra is None else spectra + term
        if d + 1 < depths:
            for i in range(parts):
                filter_of(d + 1, i)
    for b in range(beam_count):
        gain[b] = weights[b].astype(F32).reshape(2 * inputs, channels)

    section = section_ref[0]
    keep = [
        jnp.where(((section - starts[b] + sections) & (sections - 1)) < sections // 2, 1.0, 0.0)
        for b in range(beam_count)
    ]
    row = lax.broadcasted_iota(jnp.int32, (8, LANES), 0)
    low = row < 4
    even = (row & 1) == 0
    tiles = 2 * inputs // 8

    def keep_spectra(c, f, real, imag):
        for part, one, two in ((0, real, -imag), (1, imag, real)):
            mixed[c][part, f, pl.ds(0, inputs, stride=2), :] = one
            mixed[c][part, f, pl.ds(1, inputs, stride=2), :] = two

    def spectra_of(c):
        def take(r, f, part):
            at = (r * frames + f) * inputs
            lane = (2 * c + part) * LANES
            return lax.slice(spectra, (at, lane), (at + inputs, lane + LANES))

        for f in range(frames):
            keep_spectra(c, f, take(0, f, 0), take(0, f, 1))
            keep_spectra(
                c + chunks // 2, f,
                take(1, f, 0) + take(2, f, 1), take(1, f, 1) - take(2, f, 0),
            )

    for c in range(chunks // 2):
        spectra_of(c)
    per = LANES // block
    lane = lax.broadcasted_iota(jnp.int32, (1, LANES), 1)
    slot = lax.broadcasted_iota(jnp.int32, (LANES, LANES), 0)
    for c in sorted(range(chunks), key=lambda c: c % (chunks // 2)):
        for b in range(beam_count):
            gains = [gain[b, pl.ds(8 * i, 8), pl.ds(c * LANES, LANES)] for i in range(tiles)]
            for part in range(2):
                v = []
                for f in range(frames):
                    total = None
                    for i in range(tiles):
                        term = gains[i] * mixed[c][part, f, pl.ds(8 * i, 8), :]
                        total = term if total is None else total + term
                    v.append(total)
                pairs = []
                for one, two in ((v[0], v[1]), (v[2], v[3])):
                    pairs.append(
                        jnp.where(low, one, two) + pltpu.roll(jnp.where(low, two, one), 4, 0)
                    )
                one = pairs[0] + pltpu.roll(pairs[0], 7, 0)
                two = pairs[1] + pltpu.roll(pairs[1], 1, 0)
                beams[c, pl.ds(b * 16 + part * 8, 8), :] = (
                    jnp.where(even, one, two) * keep[b]
                )

        owners = owner[pl.ds(0, 1), pl.ds(c * LANES, LANES)]
        spot = (owners + (stations - LEAD_STATION % stations)) & (stations - 1)
        pick = jnp.where(slot == (lane // block) * block + spot, 1.0, 0.0).astype(BF16)
        placed = lax.dot_general(
            pick, beams[c].astype(BF16), (((1,), (1,)), ((), ())), preferred_element_type=F32
        )
        for s in range(per):
            listed = (c * per + s + sections - LEAD_SECTION % sections) % sections
            out_ref[listed] = lax.slice(
                placed, (s * block, 0), ((s + 1) * block, LANES)
            ).astype(BF16)


def place_of(beam, frame, part, pol):
    return beam * 16 + part * 8 + (frame & 1) * 4 + pol * 2 + (frame >> 1)


def selectors(beam_count, frames, stations):
    count = beam_count * frames * 2
    pick = np.zeros((2, 2, count, LANES), np.float32)
    columns = np.zeros((2, LANES, count), np.float32)
    for b in range(beam_count):
        for f in range(frames):
            for part in range(2):
                at = (b * frames + f) * 2 + part
                for pol in range(2):
                    j = place_of(b, f, part, pol)
                    pick[0, pol, at, j] = 1
                    pick[1, pol, at, place_of(b, f, 1 - part, pol)] = 1 if part else -1
                    columns[pol, j, at] = 1
    spread = np.zeros((2, stations, 2 * stations), np.float32)
    for i, station in enumerate(turned_order(stations, LEAD_STATION)):
        for pol in range(2):
            spread[pol, i, 2 * station + pol] = 1
    zero = np.zeros_like(spread)
    rows = np.stack([np.concatenate([spread, zero], 2), np.concatenate([zero, spread], 2)])
    arrays = (pick.reshape(4 * count, LANES), columns, np.swapaxes(spread, 1, 2), rows)
    return [a.astype(ml_dtypes.bfloat16) for a in arrays]


def back_kernel(dims, z_ref, pick_ref, columns_ref, spread_ref, rows_ref, out_hbm, out, sems):
    beam_count, frames, stations = dims
    count = beam_count * frames * 2
    z = z_ref[...].astype(BF16)
    turned = lax.dot_general(
        pick_ref[...], z, (((1,), (1,)), ((), ())), preferred_element_type=F32
    ).astype(BF16)
    right = None
    for side in range(2):
        for pol in range(2):
            at = (side * 2 + pol) * count
            term = jnp.dot(
                lax.slice(turned, (at, 0), (at + count, stations)), rows_ref[side, pol],
                preferred_element_type=F32,
            )
            right = term if right is None else right + term
    left = None
    for pol in range(2):
        chosen = jnp.dot(z, columns_ref[pol], preferred_element_type=F32).astype(BF16)
        term = jnp.dot(spread_ref[pol], chosen, preferred_element_type=F32)
        left = term if left is None else left + term
    upper = lax.broadcasted_iota(jnp.int32, (count, LANES), 0) < count // 2
    held = jnp.concatenate(
        [jnp.where(upper, right, 0.0), jnp.where(upper, 0.0, right)], axis=1
    ).astype(BF16)
    pair = (lax.broadcasted_iota(jnp.int32, left.shape, 1) & (count // 2 - 1)) // 2
    ends = []
    for b in range(beam_count // 2):
        streamed = jnp.concatenate(
            [jnp.where(pair == b * frames + f, left, 0.0).astype(BF16) for f in range(frames)],
            axis=0,
        )
        product = jnp.dot(streamed, held, preferred_element_type=F32).astype(BF16)
        for side in range(2):
            at = b + side * (beam_count // 2)
            for f in range(frames):
                out[at, f] = lax.slice(
                    product, (f * 2 * stations, side * LANES),
                    ((f + 1) * 2 * stations, (side + 1) * LANES),
                )
            copy = pltpu.make_async_copy(out.at[at], out_hbm.at[at], sems.at[at])
            copy.start()
            ends.append(copy)
    for copy in ends:
        copy.wait()


VMEM_SPEC = pl.BlockSpec(memory_space=pltpu.VMEM)
SMEM_SPEC = pl.BlockSpec(memory_space=pltpu.SMEM)
HBM_SPEC = pl.BlockSpec(memory_space=pltpu.HBM)


def front(sections, stations, starts, section, owner_map, taper, voltages, beam_weight_table):
    inputs = voltages.shape[1]
    taps, length = taper.shape
    frames = voltages.shape[2] // length - taps + 1
    channels = length // 2
    chunks = channels // LANES
    dims = (inputs, taps, frames, length, beam_weight_table.shape[1], sections, stations)
    return pl.pallas_call(
        functools.partial(front_kernel, dims),
        out_shape=jax.ShapeDtypeStruct((sections, channels // sections, LANES), BF16),
        in_specs=[SMEM_SPEC] + [HBM_SPEC] * 6,
        out_specs=VMEM_SPEC,
        scratch_shapes=[
            pltpu.SMEM(starts.shape, jnp.int32),
            pltpu.VMEM((1, channels), jnp.int32),
            pltpu.VMEM(taper.shape, F32),
            pltpu.VMEM((inputs, voltages.shape[2]), BF16),
            pltpu.VMEM(beam_weight_table.shape[1:], BF16),
            pltpu.VMEM((length // DEPTH, DEPTH, channels), BF16),
            pltpu.VMEM((beam_weight_table.shape[1], 2 * inputs, channels), F32),
            pltpu.VMEM((chunks, LANES, LANES), F32),
            pltpu.SemaphoreType.DMA((4 + inputs // 16 + length // DEPTH,)),
            *[pltpu.VMEM((2, frames, 2 * inputs, LANES), F32)] * chunks,
            *[pltpu.VMEM((3 * frames * inputs, DEPTH), BF16)] * (length // DEPTH),
        ],
        compiler_params=pltpu.CompilerParams(vmem_limit_bytes=16 << 20),
        name="front",
    )(
        section,
        *[
            pltpu.with_memory_space_constraint(array, pltpu.HBM)
            for array in (
                starts, owner_map.reshape(1, channels), taper, voltages, beam_weight_table,
                jnp.asarray(dft_table(length)),
            )
        ],
    )


def back(beam_count, frames, z):
    stations = z.shape[0]
    shape = (beam_count, frames, 2 * stations, 4 * stations)
    matrices = [jnp.asarray(m) for m in selectors(beam_count, frames, stations)]
    return pl.pallas_call(
        functools.partial(back_kernel, (beam_count, frames, stations)),
        out_shape=jax.ShapeDtypeStruct(shape, BF16),
        in_specs=[VMEM_SPEC] * 5,
        out_specs=HBM_SPEC,
        scratch_shapes=[pltpu.VMEM(shape, BF16), pltpu.SemaphoreType.DMA((beam_count,))],
        compiler_params=pltpu.CompilerParams(vmem_limit_bytes=16 << 20),
        name="back",
    )(z, *matrices)


def exchange(blocks, axis, lead):
    groups = [turned_order(lax.axis_size(axis), lead)]
    return lax.all_to_all(
        blocks, axis, split_axis=0, concat_axis=0, tiled=True, axis_index_groups=groups
    )


def local(voltages, taper, beam_weight_table, starts, owner_map):
    sections = lax.axis_size("section")
    stations = lax.axis_size("station")
    section = lax.axis_index("section").astype(jnp.int32).reshape(1)
    parts = front(
        sections, stations, starts, section, owner_map, taper, voltages, beam_weight_table
    )
    parts = exchange(parts, "section", LEAD_SECTION)
    total = jnp.sum(parts.astype(F32), axis=0)
    complete = exchange(total.reshape(stations, 1, LANES), "station", LEAD_STATION)
    beam_count = beam_weight_table.shape[1]
    frames = voltages.shape[2] // taper.shape[1] - taper.shape[0] + 1
    visible = back(beam_count, frames, complete.reshape(stations, LANES))
    return visible.reshape(1, 1, 1, *visible.shape)


def solution(mesh):
    placed = (
        P("station", "section", None),
        P(),
        P("station", None, "section", None, None),
        P(),
        P(),
    )
    return jax.shard_map(
        local,
        mesh=mesh,
        in_specs=placed,
        out_specs=P("section", "station", None, None, None, None, None),
        check_vma=False,
    )
```
